32 devices in a mesh: groups: 2 (over y), ctx: 4 (over z), tensor: 2 (over x), dp: 2 (over core).
Axes of the slice: x: 2, y: 2, z: 4, core: 2. Of those that a mesh axis runs over, the one named last changes fastest.
Arguments:
- tokens: bfloat16 [4, 1024, 1024], P(('groups', 'dp'), 'ctx', 'tensor'), parts along dimension 0
- w_qkv: bfloat16 [1024, 3, 1024], P(None, None, 'tensor')
- w_out: bfloat16 [1024, 1024], P('tensor'), may hold values from -0.1875 to 0.1875
- labels: int32 [4, 8, 1024], P(('groups', 'dp'), 'tensor', 'ctx'), parts along dimension 0, may hold values from 0 to 255, as said below
- grad_out: bfloat16 [4, 1024, 1024], P(('groups', 'dp'), 'ctx', 'tensor'), parts along dimension 0, may hold values from -6 to 6
Outputs:
- attended: bfloat16 [4, 1024, 1024], P(('groups', 'dp'), 'ctx', 'tensor'), parts along dimension 0
- grad_tokens: bfloat16 [4, 1024, 1024], P(('groups', 'dp'), 'ctx', 'tensor'), parts along dimension 0
- grad_w_qkv: float32 [2048, 3, 1024], P('groups', None, 'tensor'), parts along dimension 0
- grad_w_out: float32 [2048, 1024], P(('groups', 'tensor')), parts along dimension 0
The draws below stay inside these ranges and needn't reach their ends.
There are 2 independent parts, one for each index of `groups`. The reference program is written for one: setup_inputs(seed, part) draws one part's arguments, and reference() takes and returns one part's arrays. A program takes and returns all parts, laid end to end along the dimension named above; an argument that names none is the same for every part. Nothing has to cross between parts.
Inputs may be any that keep to these rules, and one draw needn't show every extreme that they name: `labels`: cluster c of any head belongs to owner c % 4. Among the 256 tokens of one document on one index of ctx, at most 192 have, for one head, clusters of one owner; for each head one owner has exactly 192 from every such block, and the other owners share the rest of a block evenly (counts differ by at most one).
All inputs are finite; a program needn't handle non-finite values.
Results may differ from the reference program's by a relative error of at most 0.035.
The reference program's roundings to bfloat16 on the way (of `qkv`, `cotangent`, `probs`, `attention`, `dscore` and `grad_qkv`) count: a program that leaves them out, or rounds other values in their place, can miss the bound.
Values may be sent and summed in bfloat16 or wider, within the bound.
A program may use at most 64 MiB of HBM per device.

```python
import math
import jax
import jax.numpy as jnp
from jax import lax

D = 1024
H = 8
HD = 128
C = 256
TOK_DEV = 256
DOCS = 2
SEQ = 1024
CAP = 192
N_CTX = 4


def draw_labels(key, part):
    base = jax.random.fold_in(key, 23)
    hottest = jax.random.randint(jax.random.fold_in(base, 1), (H,), 0, N_CTX).astype(jnp.int32)
    rank_keys = jax.random.split(jax.random.fold_in(base, 2), DOCS * H * N_CTX)
    ranks = jax.vmap(lambda one_key: jax.random.permutation(one_key, TOK_DEV))(rank_keys)
    ranks = ranks.astype(jnp.int32).reshape(DOCS, H, N_CTX, TOK_DEV)
    hot_owner = hottest[None, :, None, None]
    spread_owner = (hot_owner + 1 + jnp.maximum(ranks - CAP, 0) % (N_CTX - 1)) % N_CTX
    owner_pick = jnp.where(ranks < CAP, hot_owner, spread_owner)
    within = jax.random.randint(jax.random.fold_in(base, 3), (DOCS, H, N_CTX, TOK_DEV), 0, C // N_CTX).astype(jnp.int32)
    chosen = owner_pick + N_CTX * within
    return chosen.reshape(DOCS, H, N_CTX * TOK_DEV).astype(jnp.int32)


def draw_tokens(key, part):
    noise_key = jax.random.fold_in(key, 31)
    noise = jax.random.normal(jax.random.fold_in(noise_key, 1), (DOCS, SEQ, D), jnp.float32)
    values = noise
    return jnp.clip(values, -30.0, 30.0).astype(jnp.bfloat16)


def draw_w_qkv(key, part):
    weight_key = jax.random.fold_in(key, 47)
    fan_scale = D ** (-0.5)
    base = jax.random.normal(jax.random.fold_in(weight_key, 1), (D, 3, H * HD), jnp.float32) * fan_scale
    values = base
    return jnp.clip(values, -6.0 * fan_scale, 6.0 * fan_scale).astype(jnp.bfloat16)


def block_scale(own_key, shape, cuts, smallest, high):
    level = 1.0
    for axis_at, blocks in cuts:
        heights = jax.random.uniform(jax.random.fold_in(jax.random.fold_in(own_key, 6), axis_at), (blocks,), jnp.float32, smallest / len(cuts), high / len(cuts))
        level = level * jnp.repeat(jnp.exp(heights), shape[axis_at] // blocks).reshape((-1,) + (1,) * (len(shape) - 1 - axis_at))
    return level


def gaussian(own_key, extent, deviation, reach, shards=(), held_as=jnp.bfloat16):
    loudness = block_scale(own_key, extent, shards, -0.22, 0.18) if shards else 1.0
    values = jax.random.normal(own_key, extent, jnp.float32) * deviation * loudness
    return jnp.minimum(jnp.maximum(values, -reach), reach).astype(held_as)


def setup_inputs(seed: int = 0, part: int = 0) -> dict:
    arg_keys = jax.random.split(jax.random.key(seed), 6)
    part_splits = jax.random.split(jax.random.fold_in(arg_keys[5], part), 6)
    tokens = draw_tokens(jax.random.fold_in(jax.random.fold_in(arg_keys[5], part), 71), part)
    w_qkv = draw_w_qkv(jax.random.fold_in(arg_keys[5], 71), part)
    w_out = gaussian(arg_keys[2], (H * HD, D), (H * HD) ** -0.5, 0.1875, ((0, 2),))
    labels = draw_labels(jax.random.fold_in(jax.random.fold_in(arg_keys[5], part), 71), part)
    grad_out = gaussian(part_splits[4], (DOCS, SEQ, D), 1.0, 6.0, ((0, 2), (1, 4), (2, 2)))
    return {"tokens": tokens, "w_qkv": w_qkv, "w_out": w_out, "labels": labels, "grad_out": grad_out}


def masked_probs(query_block, label_block, keys_in, labels_in):
    scores = jnp.dot(query_block, keys_in.T, preferred_element_type=jnp.float32) * (HD ** -0.5)
    same = label_block[:, None] == labels_in[None, :]
    scores = jnp.where(same, scores, jnp.float32(-1e30))
    top_value = jnp.max(scores, axis=1, keepdims=True)
    expo = jnp.exp(scores - top_value)
    return expo / jnp.sum(expo, axis=1, keepdims=True)


def head_pass(queries, keys_in, values_in, labels_in, cotangent):
    total = queries.shape[0]
    block_rows = math.gcd(total, 512)
    block_count = total // block_rows

    def forward_block(index):
        start = index * block_rows
        query_block = lax.dynamic_slice_in_dim(queries, start, block_rows, 0)
        label_block = lax.dynamic_slice_in_dim(labels_in, start, block_rows, 0)
        probs = masked_probs(query_block, label_block, keys_in, labels_in).astype(jnp.bfloat16)
        return jnp.dot(probs, values_in, preferred_element_type=jnp.float32).astype(jnp.bfloat16)

    attention = lax.map(forward_block, jnp.arange(block_count, dtype=jnp.int32)).reshape(total, HD)

    def backward_block(carry, index):
        grad_keys, grad_values = carry
        start = index * block_rows
        query_block = lax.dynamic_slice_in_dim(queries, start, block_rows, 0)
        label_block = lax.dynamic_slice_in_dim(labels_in, start, block_rows, 0)
        attn_block = lax.dynamic_slice_in_dim(attention, start, block_rows, 0)
        cot_block = lax.dynamic_slice_in_dim(cotangent, start, block_rows, 0)
        probs_full = masked_probs(query_block, label_block, keys_in, labels_in)
        probs = probs_full.astype(jnp.bfloat16)
        dprob = jnp.dot(cot_block, values_in.T, preferred_element_type=jnp.float32)
        delta = jnp.sum(cot_block.astype(jnp.float32) * attn_block.astype(jnp.float32), axis=1, keepdims=True)
        dscore = (probs_full * (dprob - delta) * (HD ** -0.5)).astype(jnp.bfloat16)
        grad_query = jnp.dot(dscore, keys_in, preferred_element_type=jnp.float32).astype(jnp.bfloat16)
        grad_keys = grad_keys + jnp.dot(dscore.T, query_block, preferred_element_type=jnp.float32)
        grad_values = grad_values + jnp.dot(probs.T, cot_block, preferred_element_type=jnp.float32)
        return (grad_keys, grad_values), grad_query

    empty = jnp.zeros((total, HD), jnp.float32)
    (grad_keys, grad_values), grad_queries = lax.scan(backward_block, (empty, empty), jnp.arange(block_count, dtype=jnp.int32))
    return attention, grad_queries.reshape(total, HD), grad_keys.astype(jnp.bfloat16), grad_values.astype(jnp.bfloat16)


def reference(tokens, w_qkv, w_out, labels, grad_out):
    docs, seq_len, width = tokens.shape
    heads = w_out.shape[0] // HD
    flat_rows = tokens.reshape(docs * seq_len, width)
    flat_grads = grad_out.reshape(docs * seq_len, width)
    qkv = jnp.dot(flat_rows, w_qkv.reshape(width, 3 * heads * HD), preferred_element_type=jnp.float32)
    qkv = qkv.astype(jnp.bfloat16).reshape(docs, seq_len, 3, heads, HD)
    cotangent = jnp.dot(flat_grads, w_out.T, preferred_element_type=jnp.float32).astype(jnp.bfloat16)
    cotangent = cotangent.reshape(docs, seq_len, heads, HD)

    def by_head(array):
        return jnp.transpose(array, (0, 2, 1, 3)).reshape(docs * heads, seq_len, HD)

    def per_head(inputs):
        return head_pass(inputs[0], inputs[1], inputs[2], inputs[3], inputs[4])

    stacked = (by_head(qkv[:, :, 0]), by_head(qkv[:, :, 1]), by_head(qkv[:, :, 2]),
               labels.reshape(docs * heads, seq_len), by_head(cotangent))
    attention, grad_q, grad_k, grad_v = lax.map(per_head, stacked)

    def to_rows(array):
        return jnp.transpose(array.reshape(docs, heads, seq_len, HD), (0, 2, 1, 3)).reshape(docs * seq_len, heads * HD)

    attention_rows = to_rows(attention)
    attended = jnp.dot(attention_rows, w_out, preferred_element_type=jnp.float32).astype(jnp.bfloat16)
    grad_w_out = jnp.dot(attention_rows.T, flat_grads, preferred_element_type=jnp.float32)
    grad_qkv = jnp.stack([to_rows(grad_q), to_rows(grad_k), to_rows(grad_v)], axis=1).reshape(docs * seq_len, 3 * heads * HD)
    grad_w_qkv = jnp.dot(flat_rows.T, grad_qkv, preferred_element_type=jnp.float32).reshape(width, 3, heads * HD)
    grad_tokens = jnp.dot(grad_qkv, w_qkv.reshape(width, 3 * heads * HD).T, preferred_element_type=jnp.float32)
    return (attended.reshape(docs, seq_len, width), grad_tokens.astype(jnp.bfloat16).reshape(docs, seq_len, width),
            grad_w_qkv, grad_w_out)
```

```python
import functools

import jax
import jax.numpy as jnp
from jax import lax
from jax.experimental import pallas as pl
from jax.experimental.pallas import tpu as pltpu
from jax.sharding import PartitionSpec as P

HD = 128
F32 = jnp.float32
BF16 = jnp.bfloat16


def dot_general(left, right, left_dim, right_dim):
    return lax.dot_general(
        left, right, (((left_dim,), (right_dim,)), ((), ())), preferred_element_type=F32
    )


def project_kernel(rows_ref, grads_ref, w_qkv_ref, w_out_ref, out_ref):
    heads = out_ref.shape[0]
    size = heads * HD
    for j in range(3):
        part = dot_general(rows_ref[...], w_qkv_ref[:, j * size : (j + 1) * size], 1, 0).astype(BF16)
        for h in range(heads):
            out_ref[h, :, j * HD : (j + 1) * HD] = part[:, h * HD : (h + 1) * HD]
    part = dot_general(grads_ref[...], w_out_ref[...], 1, 1).astype(BF16)
    for h in range(heads):
        out_ref[h, :, 3 * HD :] = part[:, h * HD : (h + 1) * HD]


def attention_kernel(own_keys, block_rows, x_ref, kv_ref, mark_ref, key_mark_ref, *outs):
    if own_keys:
        (y_ref, gk_acc, gv_acc) = outs
        keys = x_ref[:, HD : 2 * HD]
        values = x_ref[:, 2 * HD : 3 * HD]
    else:
        (y_ref, gkv_ref, gk_acc, gv_acc) = outs
        keys = kv_ref[:, :HD]
        values = kv_ref[:, HD:]
    key_marks = key_mark_ref[...]
    count = x_ref.shape[0] // block_rows

    def one_block(b):
        rows = pl.ds(pl.multiple_of(b * block_rows, block_rows), block_rows)
        query = x_ref[rows, :HD]
        cot = x_ref[rows, 3 * HD :]
        scores = dot_general(query, keys, 1, 1) * HD ** (-0.5)
        scores = jnp.where(mark_ref[rows, :] == key_marks, scores, F32(-1e30))
        top = jnp.max(scores, axis=1, keepdims=True)
        expo = jnp.exp(scores - top)
        full = expo * (1.0 / jnp.sum(expo, axis=1, keepdims=True))
        probs = full.astype(BF16)
        attention = dot_general(probs, values, 1, 0).astype(BF16)
        dprob = dot_general(cot, values, 1, 1)
        delta = jnp.sum(cot.astype(F32) * attention.astype(F32), axis=1, keepdims=True)
        dscore = (full * (dprob - delta) * HD ** (-0.5)).astype(BF16)
        y_ref[rows, :HD] = dot_general(dscore, keys, 1, 0).astype(BF16)
        y_ref[rows, 3 * HD :] = attention
        return dot_general(dscore, query, 0, 0), dot_general(probs, cot, 0, 0)

    if count <= 4:
        grad_keys, grad_values = one_block(0)
        for b in range(1, count):
            more_keys, more_values = one_block(b)
            grad_keys = grad_keys + more_keys
            grad_values = grad_values + more_values
    else:
        gk_acc[...] = jnp.zeros_like(gk_acc)
        gv_acc[...] = jnp.zeros_like(gv_acc)

        @pl.loop(0, count)
        def _(b):
            more_keys, more_values = one_block(b)
            gk_acc[...] += more_keys
            gv_acc[...] += more_values

        grad_keys, grad_values = gk_acc[...], gv_acc[...]
    if own_keys:
        y_ref[:, HD : 2 * HD] = grad_keys.astype(BF16)
        y_ref[:, 2 * HD : 3 * HD] = grad_values.astype(BF16)
    else:
        gkv_ref[:, :HD] = grad_keys.astype(BF16)
        gkv_ref[:, HD:] = grad_values.astype(BF16)


def finish_kernel(z_ref, rows_ref, grads_ref, w_qkv_ref, w_out_ref, out_ref, in_ref, gwq_ref, gwo_ref):
    heads = z_ref.shape[0]
    size = heads * HD
    attention = jnp.concatenate([z_ref[h, :, 3 * HD :] for h in range(heads)], axis=1)
    out_ref[...] = dot_general(attention, w_out_ref[...], 1, 0).astype(BF16)
    gwo_ref[...] = dot_general(attention, grads_ref[...], 0, 0).astype(BF16)
    total = None
    for j in range(3):
        grad = jnp.concatenate([z_ref[h, :, j * HD : (j + 1) * HD] for h in range(heads)], axis=1)
        cols = slice(j * size, (j + 1) * size)
        term = dot_general(grad, w_qkv_ref[:, cols], 1, 1)
        total = term if total is None else total + term
        gwq_ref[:, cols] = dot_general(rows_ref[...], grad, 0, 0).astype(BF16)
    in_ref[...] = total.astype(BF16)


VMEM_SPEC = pl.BlockSpec(memory_space=pltpu.VMEM)


def call(kernel, shapes, scratch=(), **kw):
    return pl.pallas_call(
        kernel,
        out_shape=[jax.ShapeDtypeStruct(s, t) for s, t in shapes],
        out_specs=[VMEM_SPEC] * len(shapes),
        scratch_shapes=list(scratch),
        compiler_params=pltpu.CompilerParams(vmem_limit_bytes=56 * 2**20),
        **kw,
    )


def shards(tokens, w_qkv, w_out, labels, grad_out):
    heads = w_out.shape[0] // HD
    ctx_count = lax.axis_size("ctx")
    repeat = ctx_count // heads
    inner = [[g * heads + i for i in range(heads)] for g in range(repeat)]
    outer = [[g * heads + i for g in range(repeat)] for i in range(heads)]
    width = w_qkv.shape[0]
    size = heads * HD
    w_flat = w_qkv.reshape(width, 3 * size)

    marks_all = lax.all_gather(labels[0], "ctx", axis=1, tiled=True)
    rows = lax.all_gather(tokens, "tensor", axis=2, tiled=True)[0]
    grads = lax.all_gather(grad_out, "tensor", axis=2, tiled=True)[0]
    count = rows.shape[0]

    (packed,) = call(project_kernel, [((heads, count, 4 * HD), BF16)], in_specs=[VMEM_SPEC] * 4)(
        rows, grads, w_flat, w_out
    )
    me = lax.axis_index("ctx")
    head_of = me % heads
    exchange = functools.partial(
        lax.all_to_all, axis_name="ctx", split_axis=0, concat_axis=0, tiled=True, axis_index_groups=inner
    )
    mine = exchange(packed).reshape(heads * count, 4 * HD)
    total = heads * count
    key_marks = lax.dynamic_slice_in_dim(marks_all, head_of, 1, 0)
    row_marks = lax.dynamic_slice_in_dim(key_marks, (me // heads) * total, total, 1).reshape(total, 1)
    key_total = total * repeat
    block_rows = 256
    acc = [pltpu.VMEM((key_total, HD), F32)] * 2 if total // block_rows > 4 else [pltpu.VMEM((8, HD), F32)] * 2
    if repeat == 1:
        (back,) = call(
            functools.partial(attention_kernel, True, block_rows),
            [((total, 4 * HD), BF16)],
            acc,
            in_specs=[VMEM_SPEC] * 4,
        )(mine, mine[:8, : 2 * HD], row_marks, key_marks)
    else:
        keys_values = lax.all_gather(
            mine[:, HD : 3 * HD], "ctx", axis=0, tiled=True, axis_index_groups=outer
        )
        back, terms = call(
            functools.partial(attention_kernel, False, block_rows),
            [((total, 4 * HD), BF16), ((key_total, 2 * HD), BF16)],
            acc,
            in_specs=[VMEM_SPEC] * 4,
        )(mine, keys_values, row_marks, key_marks)
        summed = lax.psum_scatter(
            terms, "ctx", scatter_dimension=0, tiled=True, axis_index_groups=outer
        )
        back = jnp.concatenate([back[:, :HD], summed, back[:, 3 * HD :]], axis=1)
    home = exchange(back.reshape(heads, count, 4 * HD))
    out_terms, in_terms, grad_w_qkv, grad_w_out = call(
        finish_kernel,
        [
            ((count, width), BF16),
            ((count, width), BF16),
            ((width, 3 * size), BF16),
            ((size, width), BF16),
        ],
        in_specs=[VMEM_SPEC] * 5,
    )(home, rows, grads, w_flat, w_out)
    summed_qkv = lax.psum(grad_w_qkv, ("ctx", "dp")).astype(F32).reshape(width, 3, size)
    summed_out = lax.psum(grad_w_out, ("ctx", "dp")).astype(F32)
    attended = lax.psum_scatter(out_terms, "tensor", scatter_dimension=1, tiled=True)
    grad_tokens = lax.psum_scatter(in_terms, "tensor", scatter_dimension=1, tiled=True)
    return (attended[None], grad_tokens[None], summed_qkv, summed_out)


def solution(mesh):
    placed = (
        P(("groups", "dp"), "ctx", "tensor"),
        P(None, None, "tensor"),
        P("tensor", None),
        P(("groups", "dp"), "tensor", "ctx"),
        P(("groups", "dp"), "ctx", "tensor"),
    )
    return jax.shard_map(
        shards,
        mesh=mesh,
        in_specs=placed,
        out_specs=(
            P(("groups", "dp"), "ctx", "tensor"),
            P(("groups", "dp"), "ctx", "tensor"),
            P("groups", None, "tensor"),
            P(("groups", "tensor"), None),
        ),
        check_vma=False,
    )
```

```python
import functools

import jax
import jax.numpy as jnp
from jax import lax
from jax.experimental import pallas as pl
from jax.experimental.pallas import tpu as pltpu
from jax.sharding import PartitionSpec as P

HD = 128
F32 = jnp.float32
BF16 = jnp.bfloat16


def dot_general(left, right, left_dim, right_dim):
    return lax.dot_general(
        left, right, (((left_dim,), (right_dim,)), ((), ())), preferred_element_type=F32
    )


def project_kernel(rows_ref, grads_ref, w_qkv_ref, w_out_ref, out_ref):
    heads = out_ref.shape[0]
    size = heads * HD
    for j in range(3):
        part = dot_general(rows_ref[...], w_qkv_ref[:, j * size : (j + 1) * size], 1, 0).astype(BF16)
        for h in range(heads):
            out_ref[h, :, j * HD : (j + 1) * HD] = part[:, h * HD : (h + 1) * HD]
    part = dot_general(grads_ref[...], w_out_ref[...], 1, 1).astype(BF16)
    for h in range(heads):
        out_ref[h, :, 3 * HD :] = part[:, h * HD : (h + 1) * HD]


def attention_kernel(own_keys, block_rows, x_ref, kv_ref, mark_ref, key_mark_ref, *outs):
    if own_keys:
        (y_ref, gk_acc, gv_acc) = outs
        keys = x_ref[:, HD : 2 * HD]
        values = x_ref[:, 2 * HD : 3 * HD]
    else:
        (y_ref, gkv_ref, gk_acc, gv_acc) = outs
        keys = kv_ref[:, :HD]
        values = kv_ref[:, HD:]
    key_marks = key_mark_ref[...]
    count = x_ref.shape[0] // block_rows

    def one_block(b):
        rows = pl.ds(pl.multiple_of(b * block_rows, block_rows), block_rows)
        query = x_ref[rows, :HD]
        cot = x_ref[rows, 3 * HD :]
        scores = dot_general(query, keys, 1, 1) * HD ** (-0.5)
        scores = jnp.where(mark_ref[rows, :] == key_marks, scores, F32(-1e30))
        top = jnp.max(scores, axis=1, keepdims=True)
        expo = jnp.exp(scores - top)
        full = expo * (1.0 / jnp.sum(expo, axis=1, keepdims=True))
        probs = full.astype(BF16)
        attention = dot_general(probs, values, 1, 0).astype(BF16)
        dprob = dot_general(cot, values, 1, 1)
        delta = jnp.sum(cot.astype(F32) * attention.astype(F32), axis=1, keepdims=True)
        dscore = (full * (dprob - delta) * HD ** (-0.5)).astype(BF16)
        y_ref[rows, :HD] = dot_general(dscore, keys, 1, 0).astype(BF16)
        y_ref[rows, 3 * HD :] = attention
        return dot_general(dscore, query, 0, 0), dot_general(probs, cot, 0, 0)

    if count <= 4:
        grad_keys, grad_values = one_block(0)
        for b in range(1, count):
            more_keys, more_values = one_block(b)
            grad_keys = grad_keys + more_keys
            grad_values = grad_values + more_values
    else:
        gk_acc[...] = jnp.zeros_like(gk_acc)
        gv_acc[...] = jnp.zeros_like(gv_acc)

        @pl.loop(0, count)
        def _(b):
            more_keys, more_values = one_block(b)
            gk_acc[...] += more_keys
            gv_acc[...] += more_values

        grad_keys, grad_values = gk_acc[...], gv_acc[...]
    if own_keys:
        y_ref[:, HD : 2 * HD] = grad_keys.astype(BF16)
        y_ref[:, 2 * HD : 3 * HD] = grad_values.astype(BF16)
    else:
        gkv_ref[:, :HD] = grad_keys.astype(BF16)
        gkv_ref[:, HD:] = grad_values.astype(BF16)


def finish_kernel(z_ref, rows_ref, grads_ref, w_qkv_ref, w_out_ref, out_ref, in_ref, gwq_ref, gwo_ref):
    heads = z_ref.shape[0]
    size = heads * HD
    attention = jnp.concatenate([z_ref[h, :, 3 * HD :] for h in range(heads)], axis=1)
    out_ref[...] = dot_general(attention, w_out_ref[...], 1, 0).astype(BF16)
    gwo_ref[...] = dot_general(attention, grads_ref[...], 0, 0).astype(BF16)
    total = None
    for j in range(3):
        grad = jnp.concatenate([z_ref[h, :, j * HD : (j + 1) * HD] for h in range(heads)], axis=1)
        cols = slice(j * size, (j + 1) * size)
        term = dot_general(grad, w_qkv_ref[:, cols], 1, 1)
        total = term if total is None else total + term
        gwq_ref[:, cols] = dot_general(rows_ref[...], grad, 0, 0).astype(BF16)
    in_ref[...] = total.astype(BF16)


def remote(source, target, send_sem, recv_sem, device):
    return pltpu.make_async_remote_copy(
        src_ref=source,
        dst_ref=target,
        send_sem=send_sem,
        recv_sem=recv_sem,
        device_id=device,
        device_id_type=pl.DeviceIdType.MESH,
    )


def layer_kernel(
    tok_ref, gro_ref, w3_ref, wo_ref, lab_ref,
    att_out, tokgrad_out, res_out,
    rows, grads, acc, packed, heads_in, marks, full, y, home,
    part, from_core, chip_sum, from_outer, from_inner, res, x_send, x_recv, x_own, tok_out,
    sx, rx, sl, rl, sa, ra, sb, rb, su, ru, so, ro, si, ri, sq, rq, sp, rp, sc, rc, st, rt, lsem,
):
    z = lax.axis_index("ctx")
    x = lax.axis_index("tensor")
    c = lax.axis_index("dp")
    count = tok_ref.shape[0]
    half = tok_ref.shape[1]
    scale = HD ** (-0.5)
    other_x = 1 - x
    other_c = 1 - c
    x_dev = {"tensor": other_x}
    c_dev = {"dp": other_c}
    peers = [lax.rem(z + d, 4) for d in range(1, 4)]
    sources = [lax.rem(z + 4 - d, 4) for d in range(1, 4)]

    barrier = pltpu.get_barrier_semaphore()
    for device in [{"ctx": p} for p in peers] + [x_dev, c_dev]:
        pl.semaphore_signal(barrier, inc=1, device_id=device, device_id_type=pl.DeviceIdType.MESH)
    pl.semaphore_wait(barrier, 5)

    def block(index, size):
        return pl.ds(pl.multiple_of(index * size, size), size)

    x_copies = [
        remote(tok_ref, rows.at[x], sx.at[0], rx.at[0], x_dev),
        remote(gro_ref, grads.at[x], sx.at[1], rx.at[1], x_dev),
    ]
    for copy in x_copies:
        copy.start()
    label_copies = []
    for d in range(3):
        label_copies.append(
            remote(lab_ref.at[peers[d]], marks.at[z], sl.at[d], rl.at[d], {"ctx": peers[d]})
        )
        label_copies[-1].start()
    rows[x] = tok_ref[...]
    grads[x] = gro_ref[...]
    marks[z] = lab_ref[z]
    for j in range(3):
        acc[j] = dot_general(tok_ref[...], w3_ref[j, block(x, half), :], 1, 0)
    acc[3] = dot_general(gro_ref[...], wo_ref[:, block(x, half)], 1, 1)

    a_copies = []
    for j in range(4):
        if j == 0:
            x_copies[0].wait_recv()
        if j == 3:
            x_copies[1].wait_recv()
        if j < 3:
            term = dot_general(rows[other_x], w3_ref[j, block(other_x, half), :], 1, 0)
        else:
            term = dot_general(grads[other_x], wo_ref[:, block(other_x, half)], 1, 1)
        value = (acc[j] + term).astype(BF16)
        for h in range(4):
            packed[j, h] = value[:, h * HD : (h + 1) * HD]
        for d in range(3):
            copy = remote(
                packed.at[j, peers[d]],
                heads_in.at[j, block(z, count), :],
                sa.at[j, d],
                ra.at[j, d],
                {"ctx": peers[d]},
            )
            copy.start()
            a_copies.append(copy)
        heads_in[j, block(z, count), :] = packed[j, z]

    for copy in label_copies:
        copy.wait_recv()
    for copy in a_copies[:9]:
        copy.wait_recv()
    keys = heads_in[1]
    values = heads_in[2]
    key_marks = jnp.concatenate([marks[s].astype(F32) for s in range(4)], axis=1)
    order = [*peers, z]
    b_copies = []

    def send_back(j, d):
        copy = remote(
            y.at[j, block(order[d], count), :],
            home.at[j, z],
            sb.at[j, d],
            rb.at[j, d],
            {"ctx": order[d]},
        )
        copy.start()
        b_copies.append(copy)

    for d in range(4):
        here = block(order[d], count)
        mine = jnp.broadcast_to(marks[order[d]].astype(F32), (HD, count)).T[:, :1]
        scores = dot_general(heads_in[0, here, :], keys, 1, 1) * scale
        scores = jnp.where(mine == key_marks, scores, F32(-1e30))
        expo = jnp.exp(scores - jnp.max(scores, axis=1, keepdims=True))
        probs_full = expo * (1.0 / jnp.sum(expo, axis=1, keepdims=True))
        full[d] = probs_full
        y[3, here, :] = dot_general(probs_full.astype(BF16), values, 1, 0).astype(BF16)
        if d < 3:
            send_back(3, d)
    home[3, z] = y[3, block(z, count), :]
    for copy in a_copies[9:]:
        copy.wait_recv()
    grad_keys = grad_values = None
    for d in range(4):
        here = block(order[d], count)
        cot = heads_in[3, here, :]
        probs_full = full[d]
        dprob = dot_general(cot, values, 1, 1)
        delta = jnp.sum(cot.astype(F32) * y[3, here, :].astype(F32), axis=1, keepdims=True)
        dscore = (probs_full * (dprob - delta) * scale).astype(BF16)
        y[0, here, :] = dot_general(dscore, keys, 1, 0).astype(BF16)
        if d < 3:
            send_back(0, d)
        more_keys = dot_general(dscore, heads_in[0, here, :], 0, 0)
        more_values = dot_general(probs_full.astype(BF16), cot, 0, 0)
        grad_keys = more_keys if d == 0 else grad_keys + more_keys
        grad_values = more_values if d == 0 else grad_values + more_values
    home[0, z] = y[0, block(z, count), :]
    y[1] = grad_keys.astype(BF16)
    for d in range(3):
        send_back(1, d)
    home[1, z] = y[1, block(z, count), :]
    y[2] = grad_values.astype(BF16)
    for d in range(3):
        send_back(2, d)
    home[2, z] = y[2, block(z, count), :]

    b_at = {3: b_copies[0:3], 0: b_copies[3:6], 1: b_copies[6:9], 2: b_copies[9:12]}
    units = (3, 0, 1, 2)
    u_copies = {}
    kept = {}

    def unit_term(u, grad, f):
        if u == 3:
            return dot_general(grad, grads[f], 0, 0)
        return dot_general(rows[f], grad, 0, 0)

    for u in units:
        for copy in b_at[u]:
            copy.wait_recv()
        grad = jnp.concatenate([home[u, h] for h in range(4)], axis=1)
        part[u] = unit_term(u, grad, other_c).astype(BF16)
        u_copies[u] = remote(part.at[u], from_core.at[u], su.at[u], ru.at[u], c_dev)
        u_copies[u].start()
        chip_sum[u] = unit_term(u, grad, c).astype(BF16)

    inner = jnp.logical_or(z == 1, z == 2)
    side = z // 2
    inner_of_outer = jnp.where(z == 0, 1, 2)
    outer_dev = {"ctx": jnp.where(z == 1, 0, 3)}
    inner_dev = {"ctx": jnp.where(z == 1, 2, 1)}
    steps = [(u, k) for u in units for k in range(2)]

    def chunk(which, k):
        return pl.ds(pl.multiple_of(which * 256 + k * 128, 128), 128)

    def outer_send(n, which):
        u, k = steps[n]
        at = chunk(which, k)
        q = n * 2 + which
        return remote(
            chip_sum.at[u, at, :], from_outer.at[u, at, :], so.at[q], ro.at[q], {"ctx": inner_of_outer}
        )

    def from_outer_copy(n, which):
        u, k = steps[n]
        at = chunk(which, k)
        q = n * 2 + which
        return remote(chip_sum.at[u, at, :], from_outer.at[u, at, :], so.at[q], ro.at[q], outer_dev)

    def inner_partial(n, which):
        u, k = steps[n]
        at = chunk(which, k)
        return remote(chip_sum.at[u, at, :], from_inner.at[u, at, :], si.at[n], ri.at[n], inner_dev)

    def inner_result(n, which):
        u, k = steps[n]
        at = chunk(which, k)
        return remote(res.at[u, c, at, :], res.at[u, c, at, :], sq.at[n], rq.at[n], inner_dev)

    def outer_result(n, which, device):
        u, k = steps[n]
        at = chunk(which, k)
        q = n * 2 + which
        return remote(res.at[u, c, at, :], res.at[u, c, at, :], sp.at[q], rp.at[q], device)

    def core_result(n, which):
        u, k = steps[n]
        at = chunk(which, k)
        q = n * 2 + which
        return remote(res.at[u, c, at, :], res.at[u, c, at, :], sc.at[q], rc.at[q], c_dev)

    def core_result_in(n, which):
        u, k = steps[n]
        at = chunk(which, k)
        q = n * 2 + which
        return remote(res.at[u, other_c, at, :], res.at[u, other_c, at, :], sc.at[q], rc.at[q], c_dev)

    near, far = side, 1 - side
    for u in units:
        u_copies[u].wait_recv()
        chip_sum[u] = (chip_sum[u].astype(F32) + from_core[u].astype(F32)).astype(BF16)

        @pl.when(jnp.logical_not(inner))
        def _(u=u):
            for k in range(2):
                n = steps.index((u, k))
                outer_send(n, far).start()
                outer_send(n, near).start()

    t_copies = []

    def token_term(t, f):
        if t == 0:
            grad = jnp.concatenate([home[3, h] for h in range(4)], axis=1)
            return dot_general(grad, wo_ref[:, block(f, half)], 1, 0)
        total = None
        for j in range(3):
            grad = jnp.concatenate([home[j, h] for h in range(4)], axis=1)
            term = dot_general(grad, w3_ref[j, block(f, half), :], 1, 1)
            total = term if total is None else total + term
        return total

    for t in range(2):
        x_send[t] = token_term(t, other_x).astype(BF16)
        t_copies.append(remote(x_send.at[t], x_recv.at[t], st.at[t], rt.at[t], x_dev))
        t_copies[t].start()
    for t in range(2):
        x_own[t] = token_term(t, x)

    count_steps = len(steps)
    lag = 2

    @pl.when(inner)
    def _():
        def relay(n):
            inner_result(n, far).wait_recv()
            outer_result(n, far, outer_dev).start()
            core_result(n, far).start()

        for n in range(count_steps):
            u, k = steps[n]
            far_at, near_at = chunk(far, k), chunk(near, k)
            from_outer_copy(n, far).wait_recv()
            chip_sum[u, far_at, :] = (
                chip_sum[u, far_at, :].astype(F32) + from_outer[u, far_at, :].astype(F32)
            ).astype(BF16)
            inner_partial(n, far).start()
            from_outer_copy(n, near).wait_recv()
            inner_partial(n, near).wait_recv()
            res[u, c, near_at, :] = (
                chip_sum[u, near_at, :].astype(F32)
                + from_outer[u, near_at, :].astype(F32)
                + from_inner[u, near_at, :].astype(F32)
            ).astype(BF16)
            inner_result(n, near).start()
            outer_result(n, near, outer_dev).start()
            core_result(n, near).start()
            if n >= lag:
                relay(n - lag)
        for n in range(count_steps - lag, count_steps):
            relay(n)
        for n in range(count_steps):
            inner_partial(n, far).wait_send()
            inner_result(n, near).wait_send()
            for which in (near, far):
                outer_result(n, which, outer_dev).wait_send()

    @pl.when(jnp.logical_not(inner))
    def _():
        back = {"ctx": inner_of_outer}
        for n in range(count_steps):
            outer_result(n, near, back).wait_recv()
            core_result(n, near).start()
            if n >= lag:
                outer_result(n - lag, far, back).wait_recv()
                core_result(n - lag, far).start()
        for n in range(count_steps - lag, count_steps):
            outer_result(n, far, back).wait_recv()
            core_result(n, far).start()
        for n in range(count_steps):
            for which in (near, far):
                outer_send(n, which).wait_send()

    own_out = [
        pltpu.make_async_copy(res.at[u, c], res_out.at[u, c], lsem.at[u]) for u in units
    ]
    for copy in own_out:
        copy.start()
    for t in range(2):
        t_copies[t].wait_recv()
        tok_out[t] = (x_own[t].astype(BF16).astype(F32) + x_recv[t].astype(F32)).astype(BF16)
    token_out = [
        pltpu.make_async_copy(tok_out.at[0], att_out, lsem.at[8]),
        pltpu.make_async_copy(tok_out.at[1], tokgrad_out, lsem.at[9]),
    ]
    for copy in token_out:
        copy.start()
    other_out = []
    for i, u in enumerate(units):
        for n in (2 * i, 2 * i + 1):
            for which in (near, far):
                core_result_in(n, which).wait_recv()
        copy = pltpu.make_async_copy(res.at[u, other_c], res_out.at[u, other_c], lsem.at[4 + u])
        copy.start()
        other_out.append(copy)
    for copy in own_out + token_out + other_out:
        copy.wait()
    for copy in [*x_copies, *label_copies, *a_copies, *b_copies, *u_copies.values(), *t_copies]:
        copy.wait_send()
    for n in range(count_steps):
        for which in (near, far):
            core_result(n, which).wait_send()


def whole_layer(tokens, w_qkv, w_out, labels, grad_out):
    count, half = tokens.shape[1:]
    width = w_qkv.shape[0]
    size = w_out.shape[0]
    any_spec = pl.BlockSpec(memory_space=pl.ANY)
    dma = pltpu.SemaphoreType.DMA
    square = (4, half, size)
    scratch = [
        pltpu.VMEM((2, count, half), BF16),
        pltpu.VMEM((2, count, half), BF16),
        pltpu.VMEM((4, count, size), F32),
        pltpu.VMEM((4, 4, count, HD), BF16),
        pltpu.VMEM((4, 4 * count, HD), BF16),
        pltpu.VMEM((4, 1, count), jnp.int32),
        pltpu.VMEM((4, count, 4 * count), F32),
        pltpu.VMEM((4, 4 * count, HD), BF16),
        pltpu.VMEM((4, 4, count, HD), BF16),
        pltpu.VMEM(square, BF16),
        pltpu.VMEM(square, BF16),
        pltpu.VMEM(square, BF16),
        pltpu.VMEM(square, BF16),
        pltpu.VMEM(square, BF16),
        pltpu.VMEM((4, 2, half, size), BF16),
        pltpu.VMEM((2, count, half), BF16),
        pltpu.VMEM((2, count, half), BF16),
        pltpu.VMEM((2, count, half), F32),
        pltpu.VMEM((2, count, half), BF16),
    ]
    for shape in ((2,), (3,), (4, 3), (4, 3), (4,), (16,), (8,), (8,), (16,), (16,), (2,)):
        scratch += [dma(shape), dma(shape)]
    scratch.append(dma((10,)))
    attended, grad_tokens, sums = pl.pallas_call(
        layer_kernel,
        out_shape=[
            jax.ShapeDtypeStruct((count, half), BF16),
            jax.ShapeDtypeStruct((count, half), BF16),
            jax.ShapeDtypeStruct((4, 2, half, size), BF16),
        ],
        in_specs=[VMEM_SPEC] * 5,
        out_specs=[any_spec] * 3,
        scratch_shapes=scratch,
        compiler_params=pltpu.CompilerParams(
            collective_id=0, has_side_effects=True, vmem_limit_bytes=56 * 2**20
        ),
    )(tokens[0], grad_out[0], jnp.transpose(w_qkv, (1, 0, 2)), w_out, labels[0][:, None, :])
    grad_w_qkv = jnp.transpose(sums[:3].astype(F32).reshape(3, width, size), (1, 0, 2))
    grad_w_out = jnp.transpose(sums[3].astype(F32), (1, 0, 2)).reshape(size, width)
    return attended[None], grad_tokens[None], grad_w_qkv, grad_w_out


VMEM_SPEC = pl.BlockSpec(memory_space=pltpu.VMEM)


def call(kernel, shapes, scratch=(), **kw):
    return pl.pallas_call(
        kernel,
        out_shape=[jax.ShapeDtypeStruct(s, t) for s, t in shapes],
        out_specs=[VMEM_SPEC] * len(shapes),
        scratch_shapes=list(scratch),
        compiler_params=pltpu.CompilerParams(vmem_limit_bytes=56 * 2**20),
        **kw,
    )


def shards(tokens, w_qkv, w_out, labels, grad_out):
    heads = w_out.shape[0] // HD
    ctx_count = lax.axis_size("ctx")
    if (
        ctx_count == 4
        and heads == 4
        and lax.axis_size("tensor") == 2
        and lax.axis_size("dp") == 2
        and tokens.shape[1:] == (256, 512)
    ):
        return whole_layer(tokens, w_qkv, w_out, labels, grad_out)
    repeat = ctx_count // heads
    inner = [[g * heads + i for i in range(heads)] for g in range(repeat)]
    outer = [[g * heads + i for g in range(repeat)] for i in range(heads)]
    width = w_qkv.shape[0]
    size = heads * HD
    w_flat = w_qkv.reshape(width, 3 * size)

    marks_all = lax.all_gather(labels[0], "ctx", axis=1, tiled=True)
    rows = lax.all_gather(tokens, "tensor", axis=2, tiled=True)[0]
    grads = lax.all_gather(grad_out, "tensor", axis=2, tiled=True)[0]
    count = rows.shape[0]

    (packed,) = call(project_kernel, [((heads, count, 4 * HD), BF16)], in_specs=[VMEM_SPEC] * 4)(
        rows, grads, w_flat, w_out
    )
    me = lax.axis_index("ctx")
    head_of = me % heads
    exchange = functools.partial(
        lax.all_to_all, axis_name="ctx", split_axis=0, concat_axis=0, tiled=True, axis_index_groups=inner
    )
    mine = exchange(packed).reshape(heads * count, 4 * HD)
    total = heads * count
    key_marks = lax.dynamic_slice_in_dim(marks_all, head_of, 1, 0)
    row_marks = lax.dynamic_slice_in_dim(key_marks, (me // heads) * total, total, 1).reshape(total, 1)
    key_total = total * repeat
    block_rows = 256
    acc = [pltpu.VMEM((key_total, HD), F32)] * 2 if total // block_rows > 4 else [pltpu.VMEM((8, HD), F32)] * 2
    if repeat == 1:
        (back,) = call(
            functools.partial(attention_kernel, True, block_rows),
            [((total, 4 * HD), BF16)],
            acc,
            in_specs=[VMEM_SPEC] * 4,
        )(mine, mine[:8, : 2 * HD], row_marks, key_marks)
    else:
        keys_values = lax.all_gather(
            mine[:, HD : 3 * HD], "ctx", axis=0, tiled=True, axis_index_groups=outer
        )
        back, terms = call(
            functools.partial(attention_kernel, False, block_rows),
            [((total, 4 * HD), BF16), ((key_total, 2 * HD), BF16)],
            acc,
            in_specs=[VMEM_SPEC] * 4,
        )(mine, keys_values, row_marks, key_marks)
        summed = lax.psum_scatter(
            terms, "ctx", scatter_dimension=0, tiled=True, axis_index_groups=outer
        )
        back = jnp.concatenate([back[:, :HD], summed, back[:, 3 * HD :]], axis=1)
    home = exchange(back.reshape(heads, count, 4 * HD))
    out_terms, in_terms, grad_w_qkv, grad_w_out = call(
        finish_kernel,
        [
            ((count, width), BF16),
            ((count, width), BF16),
            ((width, 3 * size), BF16),
            ((size, width), BF16),
        ],
        in_specs=[VMEM_SPEC] * 5,
    )(home, rows, grads, w_flat, w_out)
    summed_qkv = lax.psum(grad_w_qkv, ("ctx", "dp")).astype(F32).reshape(width, 3, size)
    summed_out = lax.psum(grad_w_out, ("ctx", "dp")).astype(F32)
    attended = lax.psum_scatter(out_terms, "tensor", scatter_dimension=1, tiled=True)
    grad_tokens = lax.psum_scatter(in_terms, "tensor", scatter_dimension=1, tiled=True)
    return (attended[None], grad_tokens[None], summed_qkv, summed_out)


def solution(mesh):
    placed = (
        P(("groups", "dp"), "ctx", "tensor"),
        P(None, None, "tensor"),
        P("tensor", None),
        P(("groups", "dp"), "tensor", "ctx"),
        P(("groups", "dp"), "ctx", "tensor"),
    )
    return jax.shard_map(
        shards,
        mesh=mesh,
        in_specs=placed,
        out_specs=(
            P(("groups", "dp"), "ctx", "tensor"),
            P(("groups", "dp"), "ctx", "tensor"),
            P("groups", None, "tensor"),
            P(("groups", "tensor"), None),
        ),
        check_vma=False,
    )
```

```python
import functools

import jax
import jax.numpy as jnp
from jax import lax
from jax.experimental import pallas as pl
from jax.experimental.pallas import tpu as pltpu
from jax.sharding import PartitionSpec as P

HD = 128
F32 = jnp.float32
BF16 = jnp.bfloat16


def dot_general(left, right, left_dim, right_dim):
    return lax.dot_general(
        left, right, (((left_dim,), (right_dim,)), ((), ())), preferred_element_type=F32
    )


def project_kernel(rows_ref, grads_ref, w_qkv_ref, w_out_ref, out_ref):
    heads = out_ref.shape[0]
    size = heads * HD
    for j in range(3):
        part = dot_general(rows_ref[...], w_qkv_ref[:, j * size : (j + 1) * size], 1, 0).astype(BF16)
        for h in range(heads):
            out_ref[h, :, j * HD : (j + 1) * HD] = part[:, h * HD : (h + 1) * HD]
    part = dot_general(grads_ref[...], w_out_ref[...], 1, 1).astype(BF16)
    for h in range(heads):
        out_ref[h, :, 3 * HD :] = part[:, h * HD : (h + 1) * HD]


def attention_kernel(own_keys, block_rows, x_ref, kv_ref, mark_ref, key_mark_ref, *outs):
    if own_keys:
        (y_ref, gk_acc, gv_acc) = outs
        keys = x_ref[:, HD : 2 * HD]
        values = x_ref[:, 2 * HD : 3 * HD]
    else:
        (y_ref, gkv_ref, gk_acc, gv_acc) = outs
        keys = kv_ref[:, :HD]
        values = kv_ref[:, HD:]
    key_marks = key_mark_ref[...]
    count = x_ref.shape[0] // block_rows

    def one_block(b):
        rows = pl.ds(pl.multiple_of(b * block_rows, block_rows), block_rows)
        query = x_ref[rows, :HD]
        cot = x_ref[rows, 3 * HD :]
        scores = dot_general(query, keys, 1, 1) * HD ** (-0.5)
        scores = jnp.where(mark_ref[rows, :] == key_marks, scores, F32(-1e30))
        top = jnp.max(scores, axis=1, keepdims=True)
        expo = jnp.exp(scores - top)
        full = expo * (1.0 / jnp.sum(expo, axis=1, keepdims=True))
        probs = full.astype(BF16)
        attention = dot_general(probs, values, 1, 0).astype(BF16)
        dprob = dot_general(cot, values, 1, 1)
        delta = jnp.sum(cot.astype(F32) * attention.astype(F32), axis=1, keepdims=True)
        dscore = (full * (dprob - delta) * HD ** (-0.5)).astype(BF16)
        y_ref[rows, :HD] = dot_general(dscore, keys, 1, 0).astype(BF16)
        y_ref[rows, 3 * HD :] = attention
        return dot_general(dscore, query, 0, 0), dot_general(probs, cot, 0, 0)

    if count <= 4:
        grad_keys, grad_values = one_block(0)
        for b in range(1, count):
            more_keys, more_values = one_block(b)
            grad_keys = grad_keys + more_keys
            grad_values = grad_values + more_values
    else:
        gk_acc[...] = jnp.zeros_like(gk_acc)
        gv_acc[...] = jnp.zeros_like(gv_acc)

        @pl.loop(0, count)
        def _(b):
            more_keys, more_values = one_block(b)
            gk_acc[...] += more_keys
            gv_acc[...] += more_values

        grad_keys, grad_values = gk_acc[...], gv_acc[...]
    if own_keys:
        y_ref[:, HD : 2 * HD] = grad_keys.astype(BF16)
        y_ref[:, 2 * HD : 3 * HD] = grad_values.astype(BF16)
    else:
        gkv_ref[:, :HD] = grad_keys.astype(BF16)
        gkv_ref[:, HD:] = grad_values.astype(BF16)


def finish_kernel(z_ref, rows_ref, grads_ref, w_qkv_ref, w_out_ref, out_ref, in_ref, gwq_ref, gwo_ref):
    heads = z_ref.shape[0]
    size = heads * HD
    attention = jnp.concatenate([z_ref[h, :, 3 * HD :] for h in range(heads)], axis=1)
    out_ref[...] = dot_general(attention, w_out_ref[...], 1, 0).astype(BF16)
    gwo_ref[...] = dot_general(attention, grads_ref[...], 0, 0).astype(BF16)
    total = None
    for j in range(3):
        grad = jnp.concatenate([z_ref[h, :, j * HD : (j + 1) * HD] for h in range(heads)], axis=1)
        cols = slice(j * size, (j + 1) * size)
        term = dot_general(grad, w_qkv_ref[:, cols], 1, 1)
        total = term if total is None else total + term
        gwq_ref[:, cols] = dot_general(rows_ref[...], grad, 0, 0).astype(BF16)
    in_ref[...] = total.astype(BF16)


def remote(source, target, send_sem, recv_sem, device):
    return pltpu.make_async_remote_copy(
        src_ref=source,
        dst_ref=target,
        send_sem=send_sem,
        recv_sem=recv_sem,
        device_id=device,
        device_id_type=pl.DeviceIdType.MESH,
    )


def layer_kernel(
    tok_ref, gro_ref, w3_hbm, wo_hbm, lab_ref,
    att_out, tokgrad_out, gwq_out, gwo_out,
    w3_ref, wo_ref, rows, grads, acc, packed, heads_in, marks, full, y, home,
    part, from_core, chip_sum, from_outer, from_inner, res, x_send, x_recv, x_own, tok_out,
    sx, rx, sl, rl, sa, ra, sb, rb, su, ru, so, ro, si, ri, sq, rq, sp, rp, sc, rc, st, rt, lsem, wsem,
):
    z = lax.axis_index("ctx")
    x = lax.axis_index("tensor")
    c = lax.axis_index("dp")
    count = tok_ref.shape[0]
    half = tok_ref.shape[1]
    scale = HD ** (-0.5)
    other_x = 1 - x
    other_c = 1 - c
    x_dev = {"tensor": other_x}
    c_dev = {"dp": other_c}
    peers = [lax.rem(z + d, 4) for d in range(1, 4)]
    sources = [lax.rem(z + 4 - d, 4) for d in range(1, 4)]

    w_copies = [
        pltpu.make_async_copy(w3_hbm, w3_ref, wsem.at[0]),
        pltpu.make_async_copy(wo_hbm, wo_ref, wsem.at[1]),
    ]
    for copy in w_copies:
        copy.start()
    barrier = pltpu.get_barrier_semaphore()
    for device in [{"ctx": p} for p in peers] + [x_dev, c_dev]:
        pl.semaphore_signal(barrier, inc=1, device_id=device, device_id_type=pl.DeviceIdType.MESH)
    pl.semaphore_wait(barrier, 5)

    def block(index, size):
        return pl.ds(pl.multiple_of(index * size, size), size)

    pieces = 4
    piece = count // pieces
    x_copies = []
    for r in range(pieces):
        at = slice(r * piece, (r + 1) * piece)
        x_copies.append(remote(tok_ref.at[at], rows.at[x, at], sx.at[r], rx.at[r], x_dev))
    x_copies.append(remote(gro_ref, grads.at[x], sx.at[pieces], rx.at[pieces], x_dev))
    for copy in x_copies:
        copy.start()
    label_copies = []
    for d in range(3):
        label_copies.append(
            remote(lab_ref.at[peers[d]], marks.at[z], sl.at[d], rl.at[d], {"ctx": peers[d]})
        )
        label_copies[-1].start()
    rows[x] = tok_ref[...]
    grads[x] = gro_ref[...]
    marks[z] = lab_ref[z]
    for copy in w_copies:
        copy.wait()
    for j in range(3):
        acc[j] = dot_general(tok_ref[...], w3_ref[j, block(x, half), :], 1, 0)

    a_copies = []
    for r in range(pieces):
        at = slice(r * piece, (r + 1) * piece)
        x_copies[r].wait_recv()
        for j in range(3):
            term = dot_general(rows[other_x, at, :], w3_ref[j, block(other_x, half), :], 1, 0)
            value = (acc[j, at, :] + term).astype(BF16)
            for h in range(4):
                packed[h, j, at, :] = value[:, h * HD : (h + 1) * HD]
        spot = pl.ds(pl.multiple_of(z * count + r * piece, piece), piece)
        for d in range(3):
            copy = remote(
                packed.at[peers[d], 0:3, at, :],
                heads_in.at[0:3, spot, :],
                sa.at[r, d],
                ra.at[r, d],
                {"ctx": peers[d]},
            )
            copy.start()
            a_copies.append(copy)
    acc[3] = dot_general(gro_ref[...], wo_ref[:, block(x, half)], 1, 1)
    x_copies[pieces].wait_recv()
    term = dot_general(grads[other_x], wo_ref[:, block(other_x, half)], 1, 1)
    value = (acc[3] + term).astype(BF16)
    for h in range(4):
        packed[h, 3] = value[:, h * HD : (h + 1) * HD]
    for d in range(3):
        copy = remote(
            packed.at[peers[d], 3],
            heads_in.at[3, block(z, count), :],
            sa.at[pieces, d],
            ra.at[pieces, d],
            {"ctx": peers[d]},
        )
        copy.start()
        a_copies.append(copy)
    for j in range(4):
        heads_in[j, block(z, count), :] = packed[z, j]

    for copy in label_copies:
        copy.wait_recv()
    for copy in a_copies[: 3 * pieces]:
        copy.wait_recv()
    keys = heads_in[1]
    values = heads_in[2]
    key_marks = jnp.concatenate([marks[s].astype(F32) for s in range(4)], axis=1)
    order = [*peers, z]
    b_copies = []

    def send_back(j, d):
        copy = remote(
            y.at[j, block(order[d], count), :],
            home.at[j, z],
            sb.at[j, d],
            rb.at[j, d],
            {"ctx": order[d]},
        )
        copy.start()
        b_copies.append(copy)

    for d in range(4):
        here = block(order[d], count)
        mine = jnp.broadcast_to(marks[order[d]].astype(F32), (HD, count)).T[:, :1]
        scores = dot_general(heads_in[0, here, :], keys, 1, 1) * scale
        scores = jnp.where(mine == key_marks, scores, F32(-1e30))
        expo = jnp.exp(scores - jnp.max(scores, axis=1, keepdims=True))
        probs_full = expo * (1.0 / jnp.sum(expo, axis=1, keepdims=True))
        full[d] = probs_full
        y[3, here, :] = dot_general(probs_full.astype(BF16), values, 1, 0).astype(BF16)
        if d < 3:
            send_back(3, d)
    home[3, z] = y[3, block(z, count), :]
    for copy in a_copies[3 * pieces :]:
        copy.wait_recv()
    grad_keys = grad_values = None
    for d in range(4):
        here = block(order[d], count)
        cot = heads_in[3, here, :]
        probs_full = full[d]
        dprob = dot_general(cot, values, 1, 1)
        delta = jnp.sum(cot.astype(F32) * y[3, here, :].astype(F32), axis=1, keepdims=True)
        dscore = (probs_full * (dprob - delta) * scale).astype(BF16)
        y[0, here, :] = dot_general(dscore, keys, 1, 0).astype(BF16)
        if d < 3:
            send_back(0, d)
        more_keys = dot_general(dscore, heads_in[0, here, :], 0, 0)
        more_values = dot_general(probs_full.astype(BF16), cot, 0, 0)
        grad_keys = more_keys if d == 0 else grad_keys + more_keys
        grad_values = more_values if d == 0 else grad_values + more_values
    home[0, z] = y[0, block(z, count), :]
    y[1] = grad_keys.astype(BF16)
    for d in range(3):
        send_back(1, d)
    home[1, z] = y[1, block(z, count), :]
    y[2] = grad_values.astype(BF16)
    for d in range(3):
        send_back(2, d)
    home[2, z] = y[2, block(z, count), :]

    b_at = {3: b_copies[0:3], 0: b_copies[3:6], 1: b_copies[6:9], 2: b_copies[9:12]}
    units = (3, 0, 1, 2)
    u_copies = {}
    kept = {}

    def unit_term(u, grad, f):
        if u == 3:
            return dot_general(grad, grads[f], 0, 0)
        return dot_general(rows[f], grad, 0, 0)

    inner = jnp.logical_or(z == 1, z == 2)
    side = z // 2
    inner_of_outer = jnp.where(z == 0, 1, 2)
    outer_dev = {"ctx": jnp.where(z == 1, 0, 3)}
    inner_dev = {"ctx": jnp.where(z == 1, 2, 1)}
    chunks = 4
    rows_at = half // 2 // chunks
    steps = [(u, k) for u in units for k in range(chunks)]

    def chunk(which, k):
        return pl.ds(pl.multiple_of(which * (half // 2) + k * rows_at, rows_at), rows_at)

    def outer_send(n, which):
        u, k = steps[n]
        at = chunk(which, k)
        q = n * 2 + which
        return remote(
            chip_sum.at[u, at, :], from_outer.at[u, at, :], so.at[q], ro.at[q], {"ctx": inner_of_outer}
        )

    def from_outer_copy(n, which):
        u, k = steps[n]
        at = chunk(which, k)
        q = n * 2 + which
        return remote(chip_sum.at[u, at, :], from_outer.at[u, at, :], so.at[q], ro.at[q], outer_dev)

    def inner_partial(n, which):
        u, k = steps[n]
        at = chunk(which, k)
        return remote(chip_sum.at[u, at, :], from_inner.at[u, at, :], si.at[n], ri.at[n], inner_dev)

    def inner_result(n, which):
        u, k = steps[n]
        at = chunk(which, k)
        return remote(res.at[u, c, at, :], res.at[u, c, at, :], sq.at[n], rq.at[n], inner_dev)

    def outer_result(n, which, device):
        u, k = steps[n]
        at = chunk(which, k)
        q = n * 2 + which
        return remote(res.at[u, c, at, :], res.at[u, c, at, :], sp.at[q], rp.at[q], device)

    def core_result(n, which):
        u, k = steps[n]
        at = chunk(which, k)
        q = n * 2 + which
        return remote(res.at[u, c, at, :], res.at[u, c, at, :], sc.at[q], rc.at[q], c_dev)

    def core_result_in(n, which):
        u, k = steps[n]
        at = chunk(which, k)
        q = n * 2 + which
        return remote(res.at[u, other_c, at, :], res.at[u, other_c, at, :], sc.at[q], rc.at[q], c_dev)

    near, far = side, 1 - side
    def start_unit(u):
        for copy in b_at[u]:
            copy.wait_recv()
        grad = jnp.concatenate([home[u, h] for h in range(4)], axis=1)
        part[u] = unit_term(u, grad, other_c).astype(BF16)
        u_copies[u] = remote(part.at[u], from_core.at[u], su.at[u], ru.at[u], c_dev)
        u_copies[u].start()
        chip_sum[u] = unit_term(u, grad, c).astype(BF16)

    def send_unit(u):
        u_copies[u].wait_recv()
        chip_sum[u] = (chip_sum[u].astype(F32) + from_core[u].astype(F32)).astype(BF16)

        @pl.when(jnp.logical_not(inner))
        def _():
            for k in range(chunks):
                n = steps.index((u, k))
                outer_send(n, far).start()
                outer_send(n, near).start()

    start_unit(units[0])
    for before, u in zip(units, units[1:]):
        start_unit(u)
        send_unit(before)
    send_unit(units[-1])

    t_copies = []

    def token_term(t, f):
        if t == 0:
            grad = jnp.concatenate([home[3, h] for h in range(4)], axis=1)
            return dot_general(grad, wo_ref[:, block(f, half)], 1, 0)
        total = None
        for j in range(3):
            grad = jnp.concatenate([home[j, h] for h in range(4)], axis=1)
            term = dot_general(grad, w3_ref[j, block(f, half), :], 1, 1)
            total = term if total is None else total + term
        return total

    def token_piece(i):
        t = i % 2
        if i < 2:
            x_send[t] = token_term(t, other_x).astype(BF16)
            t_copies.append(remote(x_send.at[t], x_recv.at[t], st.at[t], rt.at[t], x_dev))
            t_copies[t].start()
        else:
            x_own[t] = token_term(t, x)

    count_steps = len(steps)
    lag = 2
    back = {"ctx": inner_of_outer}

    def relay(n):
        inner_result(n, far).wait_recv()
        outer_result(n, far, outer_dev).start()
        core_result(n, far).start()

    def inner_step(n):
        u, k = steps[n]
        far_at, near_at = chunk(far, k), chunk(near, k)
        from_outer_copy(n, far).wait_recv()
        chip_sum[u, far_at, :] = (
            chip_sum[u, far_at, :].astype(F32) + from_outer[u, far_at, :].astype(F32)
        ).astype(BF16)
        inner_partial(n, far).start()
        from_outer_copy(n, near).wait_recv()
        inner_partial(n, near).wait_recv()
        res[u, c, near_at, :] = (
            chip_sum[u, near_at, :].astype(F32)
            + from_outer[u, near_at, :].astype(F32)
            + from_inner[u, near_at, :].astype(F32)
        ).astype(BF16)
        inner_result(n, near).start()
        outer_result(n, near, outer_dev).start()
        core_result(n, near).start()
        if n >= lag:
            relay(n - lag)

    def outer_take(n, which):
        outer_result(n, which, back).wait_recv()
        core_result(n, which).start()

    def outer_step(n):
        outer_take(n, near)
        if n >= lag:
            outer_take(n - lag, far)

    edges = [0, 2, 4, 6, 8, count_steps]
    for i, (first, last) in enumerate(zip(edges, edges[1:])):
        final = last == count_steps

        @pl.when(inner)
        def _():
            for n in range(first, last):
                inner_step(n)
            if final:
                for n in range(count_steps - lag, count_steps):
                    relay(n)
                for n in range(count_steps):
                    inner_partial(n, far).wait_send()
                    inner_result(n, near).wait_send()
                    for which in (near, far):
                        outer_result(n, which, outer_dev).wait_send()

        @pl.when(jnp.logical_not(inner))
        def _():
            for n in range(first, last):
                outer_step(n)
            if final:
                for n in range(count_steps - lag, count_steps):
                    outer_take(n, far)
                for n in range(count_steps):
                    for which in (near, far):
                        outer_send(n, which).wait_send()

        if not final:
            token_piece(i)

    def result_out(u, f, sem):
        target = gwo_out.at[:, block(f, half)] if u == 3 else gwq_out.at[u, f]
        return pltpu.make_async_copy(res.at[u, f], target, sem)

    own_out = [
        result_out(u, c, lsem.at[u]) for u in units
    ]
    for copy in own_out:
        copy.start()
    for t in range(2):
        t_copies[t].wait_recv()
        tok_out[t] = (x_own[t].astype(BF16).astype(F32) + x_recv[t].astype(F32)).astype(BF16)
    token_out = [
        pltpu.make_async_copy(tok_out.at[0], att_out, lsem.at[8]),
        pltpu.make_async_copy(tok_out.at[1], tokgrad_out, lsem.at[9]),
    ]
    for copy in token_out:
        copy.start()
    other_out = []
    for i, u in enumerate(units):
        for n in range(chunks * i, chunks * (i + 1)):
            for which in (near, far):
                core_result_in(n, which).wait_recv()
        copy = result_out(u, other_c, lsem.at[4 + u])
        copy.start()
        other_out.append(copy)
    for copy in own_out + token_out + other_out:
        copy.wait()
    for copy in [*x_copies, *label_copies, *a_copies, *b_copies, *u_copies.values(), *t_copies]:
        copy.wait_send()
    for n in range(count_steps):
        for which in (near, far):
            core_result(n, which).wait_send()


def whole_layer(tokens, w_qkv, w_out, labels, grad_out):
    count, half = tokens.shape[1:]
    width = w_qkv.shape[0]
    size = w_out.shape[0]
    any_spec = pl.BlockSpec(memory_space=pl.ANY)
    dma = pltpu.SemaphoreType.DMA
    square = (4, half, size)
    scratch = [
        pltpu.VMEM((3, width, size), BF16),
        pltpu.VMEM((size, width), BF16),
        pltpu.VMEM((2, count, half), BF16),
        pltpu.VMEM((2, count, half), BF16),
        pltpu.VMEM((4, count, size), F32),
        pltpu.VMEM((4, 4, count, HD), BF16),
        pltpu.VMEM((4, 4 * count, HD), BF16),
        pltpu.VMEM((4, 1, count), jnp.int32),
        pltpu.VMEM((4, count, 4 * count), F32),
        pltpu.VMEM((4, 4 * count, HD), BF16),
        pltpu.VMEM((4, 4, count, HD), BF16),
        pltpu.VMEM(square, BF16),
        pltpu.VMEM(square, BF16),
        pltpu.VMEM(square, BF16),
        pltpu.VMEM(square, BF16),
        pltpu.VMEM(square, BF16),
        pltpu.VMEM((4, 2, half, size), BF16),
        pltpu.VMEM((2, count, half), BF16),
        pltpu.VMEM((2, count, half), BF16),
        pltpu.VMEM((2, count, half), F32),
        pltpu.VMEM((2, count, half), BF16),
    ]
    for shape in ((5,), (3,), (5, 3), (4, 3), (4,), (32,), (16,), (16,), (32,), (32,), (2,)):
        scratch += [dma(shape), dma(shape)]
    scratch += [dma((10,)), dma((2,))]
    attended, grad_tokens, sum_qkv, sum_out = pl.pallas_call(
        layer_kernel,
        out_shape=[
            jax.ShapeDtypeStruct((count, half), BF16),
            jax.ShapeDtypeStruct((count, half), BF16),
            jax.ShapeDtypeStruct((3, 2, half, size), BF16),
            jax.ShapeDtypeStruct((size, width), BF16),
        ],
        in_specs=[VMEM_SPEC] * 2 + [any_spec] * 2 + [VMEM_SPEC],
        out_specs=[any_spec] * 4,
        scratch_shapes=scratch,
        compiler_params=pltpu.CompilerParams(
            collective_id=0, has_side_effects=True, vmem_limit_bytes=56 * 2**20
        ),
    )(tokens[0], grad_out[0], jnp.transpose(w_qkv, (1, 0, 2)), w_out, labels[0][:, None, :])
    grad_w_qkv = jnp.transpose(sum_qkv.astype(F32).reshape(3, width, size), (1, 0, 2))
    grad_w_out = sum_out.astype(F32)
    return attended[None], grad_tokens[None], grad_w_qkv, grad_w_out


VMEM_SPEC = pl.BlockSpec(memory_space=pltpu.VMEM)


def call(kernel, shapes, scratch=(), **kw):
    return pl.pallas_call(
        kernel,
        out_shape=[jax.ShapeDtypeStruct(s, t) for s, t in shapes],
        out_specs=[VMEM_SPEC] * len(shapes),
        scratch_shapes=list(scratch),
        compiler_params=pltpu.CompilerParams(vmem_limit_bytes=56 * 2**20),
        **kw,
    )


def shards(tokens, w_qkv, w_out, labels, grad_out):
    heads = w_out.shape[0] // HD
    ctx_count = lax.axis_size("ctx")
    if (
        ctx_count == 4
        and heads == 4
        and lax.axis_size("tensor") == 2
        and lax.axis_size("dp") == 2
        and tokens.shape[1:] == (256, 512)
    ):
        return whole_layer(tokens, w_qkv, w_out, labels, grad_out)
    repeat = ctx_count // heads
    inner = [[g * heads + i for i in range(heads)] for g in range(repeat)]
    outer = [[g * heads + i for g in range(repeat)] for i in range(heads)]
    width = w_qkv.shape[0]
    size = heads * HD
    w_flat = w_qkv.reshape(width, 3 * size)

    marks_all = lax.all_gather(labels[0], "ctx", axis=1, tiled=True)
    rows = lax.all_gather(tokens, "tensor", axis=2, tiled=True)[0]
    grads = lax.all_gather(grad_out, "tensor", axis=2, tiled=True)[0]
    count = rows.shape[0]

    (packed,) = call(project_kernel, [((heads, count, 4 * HD), BF16)], in_specs=[VMEM_SPEC] * 4)(
        rows, grads, w_flat, w_out
    )
    me = lax.axis_index("ctx")
    head_of = me % heads
    exchange = functools.partial(
        lax.all_to_all, axis_name="ctx", split_axis=0, concat_axis=0, tiled=True, axis_index_groups=inner
    )
    mine = exchange(packed).reshape(heads * count, 4 * HD)
    total = heads * count
    key_marks = lax.dynamic_slice_in_dim(marks_all, head_of, 1, 0)
    row_marks = lax.dynamic_slice_in_dim(key_marks, (me // heads) * total, total, 1).reshape(total, 1)
    key_total = total * repeat
    block_rows = 256
    acc = [pltpu.VMEM((key_total, HD), F32)] * 2 if total // block_rows > 4 else [pltpu.VMEM((8, HD), F32)] * 2
    if repeat == 1:
        (back,) = call(
            functools.partial(attention_kernel, True, block_rows),
            [((total, 4 * HD), BF16)],
            acc,
            in_specs=[VMEM_SPEC] * 4,
        )(mine, mine[:8, : 2 * HD], row_marks, key_marks)
    else:
        keys_values = lax.all_gather(
            mine[:, HD : 3 * HD], "ctx", axis=0, tiled=True, axis_index_groups=outer
        )
        back, terms = call(
            functools.partial(attention_kernel, False, block_rows),
            [((total, 4 * HD), BF16), ((key_total, 2 * HD), BF16)],
            acc,
            in_specs=[VMEM_SPEC] * 4,
        )(mine, keys_values, row_marks, key_marks)
        summed = lax.psum_scatter(
            terms, "ctx", scatter_dimension=0, tiled=True, axis_index_groups=outer
        )
        back = jnp.concatenate([back[:, :HD], summed, back[:, 3 * HD :]], axis=1)
    home = exchange(back.reshape(heads, count, 4 * HD))
    out_terms, in_terms, grad_w_qkv, grad_w_out = call(
        finish_kernel,
        [
            ((count, width), BF16),
            ((count, width), BF16),
            ((width, 3 * size), BF16),
            ((size, width), BF16),
        ],
        in_specs=[VMEM_SPEC] * 5,
    )(home, rows, grads, w_flat, w_out)
    summed_qkv = lax.psum(grad_w_qkv, ("ctx", "dp")).astype(F32).reshape(width, 3, size)
    summed_out = lax.psum(grad_w_out, ("ctx", "dp")).astype(F32)
    attended = lax.psum_scatter(out_terms, "tensor", scatter_dimension=1, tiled=True)
    grad_tokens = lax.psum_scatter(in_terms, "tensor", scatter_dimension=1, tiled=True)
    return (attended[None], grad_tokens[None], summed_qkv, summed_out)


def solution(mesh):
    placed = (
        P(("groups", "dp"), "ctx", "tensor"),
        P(None, None, "tensor"),
        P("tensor", None),
        P(("groups", "dp"), "tensor", "ctx"),
        P(("groups", "dp"), "ctx", "tensor"),
    )
    return jax.shard_map(
        shards,
        mesh=mesh,
        in_specs=placed,
        out_specs=(
            P(("groups", "dp"), "ctx", "tensor"),
            P(("groups", "dp"), "ctx", "tensor"),
            P("groups", None, "tensor"),
            P(("groups", "tensor"), None),
        ),
        check_vma=False,
    )
```

```python
import functools

import jax
import jax.numpy as jnp
from jax import lax
from jax.experimental import pallas as pl
from jax.experimental.pallas import tpu as pltpu
from jax.sharding import PartitionSpec as P

HD = 128
F32 = jnp.float32
BF16 = jnp.bfloat16


def dot_general(left, right, left_dim, right_dim):
    return lax.dot_general(
        left, right, (((left_dim,), (right_dim,)), ((), ())), preferred_element_type=F32
    )


def project_kernel(rows_ref, grads_ref, w_qkv_ref, w_out_ref, out_ref):
    heads = out_ref.shape[0]
    size = heads * HD
    for j in range(3):
        part = dot_general(rows_ref[...], w_qkv_ref[:, j * size : (j + 1) * size], 1, 0).astype(BF16)
        for h in range(heads):
            out_ref[h, :, j * HD : (j + 1) * HD] = part[:, h * HD : (h + 1) * HD]
    part = dot_general(grads_ref[...], w_out_ref[...], 1, 1).astype(BF16)
    for h in range(heads):
        out_ref[h, :, 3 * HD :] = part[:, h * HD : (h + 1) * HD]


def attention_kernel(own_keys, block_rows, x_ref, kv_ref, mark_ref, key_mark_ref, *outs):
    if own_keys:
        (y_ref, gk_acc, gv_acc) = outs
        keys = x_ref[:, HD : 2 * HD]
        values = x_ref[:, 2 * HD : 3 * HD]
    else:
        (y_ref, gkv_ref, gk_acc, gv_acc) = outs
        keys = kv_ref[:, :HD]
        values = kv_ref[:, HD:]
    key_marks = key_mark_ref[...]
    count = x_ref.shape[0] // block_rows

    def one_block(b):
        rows = pl.ds(pl.multiple_of(b * block_rows, block_rows), block_rows)
        query = x_ref[rows, :HD]
        cot = x_ref[rows, 3 * HD :]
        scores = dot_general(query, keys, 1, 1) * HD ** (-0.5)
        scores = jnp.where(mark_ref[rows, :] == key_marks, scores, F32(-1e30))
        top = jnp.max(scores, axis=1, keepdims=True)
        expo = jnp.exp(scores - top)
        full = expo * (1.0 / jnp.sum(expo, axis=1, keepdims=True))
        probs = full.astype(BF16)
        attention = dot_general(probs, values, 1, 0).astype(BF16)
        dprob = dot_general(cot, values, 1, 1)
        delta = jnp.sum(cot.astype(F32) * attention.astype(F32), axis=1, keepdims=True)
        dscore = (full * (dprob - delta) * HD ** (-0.5)).astype(BF16)
        y_ref[rows, :HD] = dot_general(dscore, keys, 1, 0).astype(BF16)
        y_ref[rows, 3 * HD :] = attention
        return dot_general(dscore, query, 0, 0), dot_general(probs, cot, 0, 0)

    if count <= 4:
        grad_keys, grad_values = one_block(0)
        for b in range(1, count):
            more_keys, more_values = one_block(b)
            grad_keys = grad_keys + more_keys
            grad_values = grad_values + more_values
    else:
        gk_acc[...] = jnp.zeros_like(gk_acc)
        gv_acc[...] = jnp.zeros_like(gv_acc)

        @pl.loop(0, count)
        def _(b):
            more_keys, more_values = one_block(b)
            gk_acc[...] += more_keys
            gv_acc[...] += more_values

        grad_keys, grad_values = gk_acc[...], gv_acc[...]
    if own_keys:
        y_ref[:, HD : 2 * HD] = grad_keys.astype(BF16)
        y_ref[:, 2 * HD : 3 * HD] = grad_values.astype(BF16)
    else:
        gkv_ref[:, :HD] = grad_keys.astype(BF16)
        gkv_ref[:, HD:] = grad_values.astype(BF16)


def finish_kernel(z_ref, rows_ref, grads_ref, w_qkv_ref, w_out_ref, out_ref, in_ref, gwq_ref, gwo_ref):
    heads = z_ref.shape[0]
    size = heads * HD
    attention = jnp.concatenate([z_ref[h, :, 3 * HD :] for h in range(heads)], axis=1)
    out_ref[...] = dot_general(attention, w_out_ref[...], 1, 0).astype(BF16)
    gwo_ref[...] = dot_general(attention, grads_ref[...], 0, 0).astype(BF16)
    total = None
    for j in range(3):
        grad = jnp.concatenate([z_ref[h, :, j * HD : (j + 1) * HD] for h in range(heads)], axis=1)
        cols = slice(j * size, (j + 1) * size)
        term = dot_general(grad, w_qkv_ref[:, cols], 1, 1)
        total = term if total is None else total + term
        gwq_ref[:, cols] = dot_general(rows_ref[...], grad, 0, 0).astype(BF16)
    in_ref[...] = total.astype(BF16)


def remote(source, target, send_sem, recv_sem, device):
    return pltpu.make_async_remote_copy(
        src_ref=source,
        dst_ref=target,
        send_sem=send_sem,
        recv_sem=recv_sem,
        device_id=device,
        device_id_type=pl.DeviceIdType.MESH,
    )


def layer_kernel(
    tok_ref, gro_ref, w3_hbm, wo_hbm, lab_ref,
    att_out, tokgrad_out, gwq_out, gwo_out,
    w3_ref, wo_ref, rows, grads, acc, packed, heads_in, marks, full, y, home,
    part, from_core, chip_sum, from_outer, from_inner, res, x_send, x_recv, x_own, tok_out,
    sx, rx, sl, rl, sa, ra, sb, rb, su, ru, so, ro, si, ri, sq, rq, sp, rp, sc, rc, st, rt, lsem, wsem,
):
    z = lax.axis_index("ctx")
    x = lax.axis_index("tensor")
    c = lax.axis_index("dp")
    count = tok_ref.shape[0]
    half = tok_ref.shape[1]
    scale = HD ** (-0.5)
    other_x = 1 - x
    other_c = 1 - c
    x_dev = {"tensor": other_x}
    c_dev = {"dp": other_c}
    peers = [lax.rem(z + d, 4) for d in range(1, 4)]
    sources = [lax.rem(z + 4 - d, 4) for d in range(1, 4)]

    w_copies = [
        pltpu.make_async_copy(w3_hbm, w3_ref, wsem.at[0]),
        pltpu.make_async_copy(wo_hbm, wo_ref, wsem.at[1]),
    ]
    for copy in w_copies:
        copy.start()
    barrier = pltpu.get_barrier_semaphore()
    for device in [{"ctx": p} for p in peers] + [x_dev, c_dev]:
        pl.semaphore_signal(barrier, inc=1, device_id=device, device_id_type=pl.DeviceIdType.MESH)
    pl.semaphore_wait(barrier, 5)

    def block(index, size):
        return pl.ds(pl.multiple_of(index * size, size), size)

    pieces = 4
    piece = count // pieces
    x_copies = []
    for r in range(pieces):
        at = slice(r * piece, (r + 1) * piece)
        x_copies.append(remote(tok_ref.at[at], rows.at[x, at], sx.at[r], rx.at[r], x_dev))
    x_copies.append(remote(gro_ref, grads.at[x], sx.at[pieces], rx.at[pieces], x_dev))
    for copy in x_copies:
        copy.start()
    label_copies = []
    for d in range(3):
        label_copies.append(
            remote(lab_ref.at[peers[d]], marks.at[z], sl.at[d], rl.at[d], {"ctx": peers[d]})
        )
        label_copies[-1].start()
    rows[x] = tok_ref[...]
    grads[x] = gro_ref[...]
    marks[z] = lab_ref[z]
    for copy in w_copies:
        copy.wait()
    for j in range(3):
        acc[j] = dot_general(tok_ref[...], w3_ref[j, block(x, half), :], 1, 0)

    a_copies = []
    for r in range(pieces):
        at = slice(r * piece, (r + 1) * piece)
        x_copies[r].wait_recv()
        for j in range(3):
            term = dot_general(rows[other_x, at, :], w3_ref[j, block(other_x, half), :], 1, 0)
            value = (acc[j, at, :] + term).astype(BF16)
            for h in range(4):
                packed[h, j, at, :] = value[:, h * HD : (h + 1) * HD]
        spot = pl.ds(pl.multiple_of(z * count + r * piece, piece), piece)
        for d in range(3):
            copy = remote(
                packed.at[peers[d], 0:3, at, :],
                heads_in.at[0:3, spot, :],
                sa.at[r, d],
                ra.at[r, d],
                {"ctx": peers[d]},
            )
            copy.start()
            a_copies.append(copy)
    acc[3] = dot_general(gro_ref[...], wo_ref[:, block(x, half)], 1, 1)
    x_copies[pieces].wait_recv()
    term = dot_general(grads[other_x], wo_ref[:, block(other_x, half)], 1, 1)
    value = (acc[3] + term).astype(BF16)
    for h in range(4):
        packed[h, 3] = value[:, h * HD : (h + 1) * HD]
    for d in range(3):
        copy = remote(
            packed.at[peers[d], 3],
            heads_in.at[3, block(z, count), :],
            sa.at[pieces, d],
            ra.at[pieces, d],
            {"ctx": peers[d]},
        )
        copy.start()
        a_copies.append(copy)
    for j in range(4):
        heads_in[j, block(z, count), :] = packed[z, j]

    for copy in label_copies:
        copy.wait_recv()
    for copy in a_copies[: 3 * pieces]:
        copy.wait_recv()
    keys = heads_in[1]
    values = heads_in[2]
    key_marks = jnp.concatenate([marks[s].astype(F32) for s in range(4)], axis=1)
    order = [*peers, z]
    b_copies = []

    def send_back(j, d):
        copy = remote(
            y.at[j, block(order[d], count), :],
            home.at[j, z],
            sb.at[j, d],
            rb.at[j, d],
            {"ctx": order[d]},
        )
        copy.start()
        b_copies.append(copy)

    for d in range(4):
        here = block(order[d], count)
        mine = jnp.broadcast_to(marks[order[d]].astype(F32), (HD, count)).T[:, :1]
        scores = dot_general(heads_in[0, here, :], keys, 1, 1) * scale
        scores = jnp.where(mine == key_marks, scores, F32(-1e30))
        expo = jnp.exp(scores - jnp.max(scores, axis=1, keepdims=True))
        probs_full = expo * (1.0 / jnp.sum(expo, axis=1, keepdims=True))
        full[d] = probs_full
        y[3, here, :] = dot_general(probs_full.astype(BF16), values, 1, 0).astype(BF16)
        if d < 3:
            send_back(3, d)
    home[3, z] = y[3, block(z, count), :]
    for copy in a_copies[3 * pieces :]:
        copy.wait_recv()
    grad_keys = grad_values = None
    for d in range(4):
        here = block(order[d], count)
        cot = heads_in[3, here, :]
        probs_full = full[d]
        dprob = dot_general(cot, values, 1, 1)
        delta = jnp.sum(cot.astype(F32) * y[3, here, :].astype(F32), axis=1, keepdims=True)
        dscore = (probs_full * (dprob - delta) * scale).astype(BF16)
        y[0, here, :] = dot_general(dscore, keys, 1, 0).astype(BF16)
        if d < 3:
            send_back(0, d)
        more_keys = dot_general(dscore, heads_in[0, here, :], 0, 0)
        more_values = dot_general(probs_full.astype(BF16), cot, 0, 0)
        grad_keys = more_keys if d == 0 else grad_keys + more_keys
        grad_values = more_values if d == 0 else grad_values + more_values
    home[0, z] = y[0, block(z, count), :]
    y[1] = grad_keys.astype(BF16)
    for d in range(3):
        send_back(1, d)
    home[1, z] = y[1, block(z, count), :]
    y[2] = grad_values.astype(BF16)
    for d in range(3):
        send_back(2, d)
    home[2, z] = y[2, block(z, count), :]

    b_at = {3: b_copies[0:3], 0: b_copies[3:6], 1: b_copies[6:9], 2: b_copies[9:12]}
    units = (3, 0, 1, 2)
    u_copies = {}
    kept = {}

    def unit_term(u, grad, f):
        if u == 3:
            return dot_general(grad, grads[f], 0, 0)
        return dot_general(rows[f], grad, 0, 0)

    inner = jnp.logical_or(z == 1, z == 2)
    side = z // 2
    inner_of_outer = jnp.where(z == 0, 1, 2)
    outer_dev = {"ctx": jnp.where(z == 1, 0, 3)}
    inner_dev = {"ctx": jnp.where(z == 1, 2, 1)}
    chunks = 1
    rows_at = half // 2 // chunks
    steps = [(u, k) for u in units for k in range(chunks)]

    def chunk(which, k):
        return pl.ds(pl.multiple_of(which * (half // 2) + k * rows_at, rows_at), rows_at)

    def outer_send(n, which):
        u, k = steps[n]
        at = chunk(which, k)
        q = n * 2 + which
        return remote(
            chip_sum.at[u, at, :], from_outer.at[u, at, :], so.at[q], ro.at[q], {"ctx": inner_of_outer}
        )

    def from_outer_copy(n, which):
        u, k = steps[n]
        at = chunk(which, k)
        q = n * 2 + which
        return remote(chip_sum.at[u, at, :], from_outer.at[u, at, :], so.at[q], ro.at[q], outer_dev)

    def inner_partial(n, which):
        u, k = steps[n]
        at = chunk(which, k)
        return remote(chip_sum.at[u, at, :], from_inner.at[u, at, :], si.at[n], ri.at[n], inner_dev)

    def inner_result(n, which):
        u, k = steps[n]
        at = chunk(which, k)
        return remote(res.at[u, c, at, :], res.at[u, c, at, :], sq.at[n], rq.at[n], inner_dev)

    def outer_result(n, which, device):
        u, k = steps[n]
        at = chunk(which, k)
        q = n * 2 + which
        return remote(res.at[u, c, at, :], res.at[u, c, at, :], sp.at[q], rp.at[q], device)

    def core_result(n, which):
        u, k = steps[n]
        at = chunk(which, k)
        q = n * 2 + which
        return remote(res.at[u, c, at, :], res.at[u, c, at, :], sc.at[q], rc.at[q], c_dev)

    def core_result_in(n, which):
        u, k = steps[n]
        at = chunk(which, k)
        q = n * 2 + which
        return remote(res.at[u, other_c, at, :], res.at[u, other_c, at, :], sc.at[q], rc.at[q], c_dev)

    near, far = side, 1 - side
    def start_unit(u):
        for copy in b_at[u]:
            copy.wait_recv()
        grad = jnp.concatenate([home[u, h] for h in range(4)], axis=1)
        part[u] = unit_term(u, grad, other_c).astype(BF16)
        u_copies[u] = remote(part.at[u], from_core.at[u], su.at[u], ru.at[u], c_dev)
        u_copies[u].start()
        chip_sum[u] = unit_term(u, grad, c).astype(BF16)

    def send_unit(u):
        u_copies[u].wait_recv()
        chip_sum[u] = (chip_sum[u].astype(F32) + from_core[u].astype(F32)).astype(BF16)

        @pl.when(jnp.logical_not(inner))
        def _():
            for k in range(chunks):
                n = steps.index((u, k))
                outer_send(n, far).start()
                outer_send(n, near).start()

    start_unit(units[0])
    for before, u in zip(units, units[1:]):
        start_unit(u)
        send_unit(before)
    send_unit(units[-1])

    t_copies = []

    def token_term(t, f):
        if t == 0:
            grad = jnp.concatenate([home[3, h] for h in range(4)], axis=1)
            return dot_general(grad, wo_ref[:, block(f, half)], 1, 0)
        total = None
        for j in range(3):
            grad = jnp.concatenate([home[j, h] for h in range(4)], axis=1)
            term = dot_general(grad, w3_ref[j, block(f, half), :], 1, 1)
            total = term if total is None else total + term
        return total

    def token_piece(i):
        t = i % 2
        if i < 2:
            x_send[t] = token_term(t, other_x).astype(BF16)
            t_copies.append(remote(x_send.at[t], x_recv.at[t], st.at[t], rt.at[t], x_dev))
            t_copies[t].start()
        else:
            x_own[t] = token_term(t, x)

    count_steps = len(steps)
    lag = 1
    back = {"ctx": inner_of_outer}

    def relay(n):
        inner_result(n, far).wait_recv()
        outer_result(n, far, outer_dev).start()
        core_result(n, far).start()

    def inner_step(n):
        u, k = steps[n]
        far_at, near_at = chunk(far, k), chunk(near, k)
        from_outer_copy(n, far).wait_recv()
        chip_sum[u, far_at, :] = (
            chip_sum[u, far_at, :].astype(F32) + from_outer[u, far_at, :].astype(F32)
        ).astype(BF16)
        inner_partial(n, far).start()
        from_outer_copy(n, near).wait_recv()
        inner_partial(n, near).wait_recv()
        res[u, c, near_at, :] = (
            chip_sum[u, near_at, :].astype(F32)
            + from_outer[u, near_at, :].astype(F32)
            + from_inner[u, near_at, :].astype(F32)
        ).astype(BF16)
        inner_result(n, near).start()
        outer_result(n, near, outer_dev).start()
        core_result(n, near).start()
        if n >= lag:
            relay(n - lag)

    def outer_take(n, which):
        outer_result(n, which, back).wait_recv()
        core_result(n, which).start()

    def outer_step(n):
        outer_take(n, near)
        if n >= lag:
            outer_take(n - lag, far)

    edges = [0, 0, 1, 2, 3, count_steps]
    for i, (first, last) in enumerate(zip(edges, edges[1:])):
        final = last == count_steps

        @pl.when(inner)
        def _():
            for n in range(first, last):
                inner_step(n)
            if final:
                for n in range(count_steps - lag, count_steps):
                    relay(n)
                for n in range(count_steps):
                    inner_partial(n, far).wait_send()
                    inner_result(n, near).wait_send()
                    for which in (near, far):
                        outer_result(n, which, outer_dev).wait_send()

        @pl.when(jnp.logical_not(inner))
        def _():
            for n in range(first, last):
                outer_step(n)
            if final:
                for n in range(count_steps - lag, count_steps):
                    outer_take(n, far)
                for n in range(count_steps):
                    for which in (near, far):
                        outer_send(n, which).wait_send()

        if not final:
            token_piece(i)

    def result_out(u, f, sem):
        target = gwo_out.at[:, block(f, half)] if u == 3 else gwq_out.at[u, f]
        return pltpu.make_async_copy(res.at[u, f], target, sem)

    own_out = [
        result_out(u, c, lsem.at[u]) for u in units
    ]
    for copy in own_out:
        copy.start()
    for t in range(2):
        t_copies[t].wait_recv()
        tok_out[t] = (x_own[t].astype(BF16).astype(F32) + x_recv[t].astype(F32)).astype(BF16)
    token_out = [
        pltpu.make_async_copy(tok_out.at[0], att_out, lsem.at[8]),
        pltpu.make_async_copy(tok_out.at[1], tokgrad_out, lsem.at[9]),
    ]
    for copy in token_out:
        copy.start()
    other_out = []
    for i, u in enumerate(units):
        for n in range(chunks * i, chunks * (i + 1)):
            for which in (near, far):
                core_result_in(n, which).wait_recv()
        copy = result_out(u, other_c, lsem.at[4 + u])
        copy.start()
        other_out.append(copy)
    for copy in own_out + token_out + other_out:
        copy.wait()
    for copy in [*x_copies, *label_copies, *a_copies, *b_copies, *u_copies.values(), *t_copies]:
        copy.wait_send()
    for n in range(count_steps):
        for which in (near, far):
            core_result(n, which).wait_send()


def whole_layer(tokens, w_qkv, w_out, labels, grad_out):
    count, half = tokens.shape[1:]
    width = w_qkv.shape[0]
    size = w_out.shape[0]
    any_spec = pl.BlockSpec(memory_space=pl.ANY)
    dma = pltpu.SemaphoreType.DMA
    square = (4, half, size)
    scratch = [
        pltpu.VMEM((3, width, size), BF16),
        pltpu.VMEM((size, width), BF16),
        pltpu.VMEM((2, count, half), BF16),
        pltpu.VMEM((2, count, half), BF16),
        pltpu.VMEM((4, count, size), F32),
        pltpu.VMEM((4, 4, count, HD), BF16),
        pltpu.VMEM((4, 4 * count, HD), BF16),
        pltpu.VMEM((4, 1, count), jnp.int32),
        pltpu.VMEM((4, count, 4 * count), F32),
        pltpu.VMEM((4, 4 * count, HD), BF16),
        pltpu.VMEM((4, 4, count, HD), BF16),
        pltpu.VMEM(square, BF16),
        pltpu.VMEM(square, BF16),
        pltpu.VMEM(square, BF16),
        pltpu.VMEM(square, BF16),
        pltpu.VMEM(square, BF16),
        pltpu.VMEM((4, 2, half, size), BF16),
        pltpu.VMEM((2, count, half), BF16),
        pltpu.VMEM((2, count, half), BF16),
        pltpu.VMEM((2, count, half), F32),
        pltpu.VMEM((2, count, half), BF16),
    ]
    for shape in ((5,), (3,), (5, 3), (4, 3), (4,), (32,), (16,), (16,), (32,), (32,), (2,)):
        scratch += [dma(shape), dma(shape)]
    scratch += [dma((10,)), dma((2,))]
    attended, grad_tokens, sum_qkv, sum_out = pl.pallas_call(
        layer_kernel,
        out_shape=[
            jax.ShapeDtypeStruct((count, half), BF16),
            jax.ShapeDtypeStruct((count, half), BF16),
            jax.ShapeDtypeStruct((3, 2, half, size), BF16),
            jax.ShapeDtypeStruct((size, width), BF16),
        ],
        in_specs=[VMEM_SPEC] * 2 + [any_spec] * 2 + [VMEM_SPEC],
        out_specs=[any_spec] * 4,
        scratch_shapes=scratch,
        compiler_params=pltpu.CompilerParams(
            collective_id=0, has_side_effects=True, vmem_limit_bytes=56 * 2**20
        ),
    )(tokens[0], grad_out[0], jnp.transpose(w_qkv, (1, 0, 2)), w_out, labels[0][:, None, :])
    grad_w_qkv = jnp.transpose(sum_qkv.astype(F32).reshape(3, width, size), (1, 0, 2))
    grad_w_out = sum_out.astype(F32)
    return attended[None], grad_tokens[None], grad_w_qkv, grad_w_out


VMEM_SPEC = pl.BlockSpec(memory_space=pltpu.VMEM)


def call(kernel, shapes, scratch=(), **kw):
    return pl.pallas_call(
        kernel,
        out_shape=[jax.ShapeDtypeStruct(s, t) for s, t in shapes],
        out_specs=[VMEM_SPEC] * len(shapes),
        scratch_shapes=list(scratch),
        compiler_params=pltpu.CompilerParams(vmem_limit_bytes=56 * 2**20),
        **kw,
    )


def shards(tokens, w_qkv, w_out, labels, grad_out):
    heads = w_out.shape[0] // HD
    ctx_count = lax.axis_size("ctx")
    if (
        ctx_count == 4
        and heads == 4
        and lax.axis_size("tensor") == 2
        and lax.axis_size("dp") == 2
        and tokens.shape[1:] == (256, 512)
    ):
        return whole_layer(tokens, w_qkv, w_out, labels, grad_out)
    repeat = ctx_count // heads
    inner = [[g * heads + i for i in range(heads)] for g in range(repeat)]
    outer = [[g * heads + i for g in range(repeat)] for i in range(heads)]
    width = w_qkv.shape[0]
    size = heads * HD
    w_flat = w_qkv.reshape(width, 3 * size)

    marks_all = lax.all_gather(labels[0], "ctx", axis=1, tiled=True)
    rows = lax.all_gather(tokens, "tensor", axis=2, tiled=True)[0]
    grads = lax.all_gather(grad_out, "tensor", axis=2, tiled=True)[0]
    count = rows.shape[0]

    (packed,) = call(project_kernel, [((heads, count, 4 * HD), BF16)], in_specs=[VMEM_SPEC] * 4)(
        rows, grads, w_flat, w_out
    )
    me = lax.axis_index("ctx")
    head_of = me % heads
    exchange = functools.partial(
        lax.all_to_all, axis_name="ctx", split_axis=0, concat_axis=0, tiled=True, axis_index_groups=inner
    )
    mine = exchange(packed).reshape(heads * count, 4 * HD)
    total = heads * count
    key_marks = lax.dynamic_slice_in_dim(marks_all, head_of, 1, 0)
    row_marks = lax.dynamic_slice_in_dim(key_marks, (me // heads) * total, total, 1).reshape(total, 1)
    key_total = total * repeat
    block_rows = 256
    acc = [pltpu.VMEM((key_total, HD), F32)] * 2 if total // block_rows > 4 else [pltpu.VMEM((8, HD), F32)] * 2
    if repeat == 1:
        (back,) = call(
            functools.partial(attention_kernel, True, block_rows),
            [((total, 4 * HD), BF16)],
            acc,
            in_specs=[VMEM_SPEC] * 4,
        )(mine, mine[:8, : 2 * HD], row_marks, key_marks)
    else:
        keys_values = lax.all_gather(
            mine[:, HD : 3 * HD], "ctx", axis=0, tiled=True, axis_index_groups=outer
        )
        back, terms = call(
            functools.partial(attention_kernel, False, block_rows),
            [((total, 4 * HD), BF16), ((key_total, 2 * HD), BF16)],
            acc,
            in_specs=[VMEM_SPEC] * 4,
        )(mine, keys_values, row_marks, key_marks)
        summed = lax.psum_scatter(
            terms, "ctx", scatter_dimension=0, tiled=True, axis_index_groups=outer
        )
        back = jnp.concatenate([back[:, :HD], summed, back[:, 3 * HD :]], axis=1)
    home = exchange(back.reshape(heads, count, 4 * HD))
    out_terms, in_terms, grad_w_qkv, grad_w_out = call(
        finish_kernel,
        [
            ((count, width), BF16),
            ((count, width), BF16),
            ((width, 3 * size), BF16),
            ((size, width), BF16),
        ],
        in_specs=[VMEM_SPEC] * 5,
    )(home, rows, grads, w_flat, w_out)
    summed_qkv = lax.psum(grad_w_qkv, ("ctx", "dp")).astype(F32).reshape(width, 3, size)
    summed_out = lax.psum(grad_w_out, ("ctx", "dp")).astype(F32)
    attended = lax.psum_scatter(out_terms, "tensor", scatter_dimension=1, tiled=True)
    grad_tokens = lax.psum_scatter(in_terms, "tensor", scatter_dimension=1, tiled=True)
    return (attended[None], grad_tokens[None], summed_qkv, summed_out)


def solution(mesh):
    placed = (
        P(("groups", "dp"), "ctx", "tensor"),
        P(None, None, "tensor"),
        P("tensor", None),
        P(("groups", "dp"), "tensor", "ctx"),
        P(("groups", "dp"), "ctx", "tensor"),
    )
    return jax.shard_map(
        shards,
        mesh=mesh,
        in_specs=placed,
        out_specs=(
            P(("groups", "dp"), "ctx", "tensor"),
            P(("groups", "dp"), "ctx", "tensor"),
            P("groups", None, "tensor"),
            P(("groups", "tensor"), None),
        ),
        check_vma=False,
    )
```
